32 devices in a mesh: fold: 2 (over y), vox: 16 (over z, x, core).
Axes of the slice: x: 2, y: 2, z: 4, core: 2. Of those that a mesh axis runs over, the one named last changes fastest.
Arguments:
- volumes: float32 [1024, 12288], P('fold', 'vox'), parts along dimension 0, may hold values from -6 to 6
- record_index: int32 [512], P('fold'), parts along dimension 0, may hold values from 0 to 511
- fold_of: int32 [1024], P('fold'), parts along dimension 0, may hold values from 0 to 4
- held_out: int32 [2], P('fold'), parts along dimension 0, may hold values from 0 to 4
- dictionary: float32 [12288, 512], P('vox'), may hold values from -1 to 1
Outputs:
- new_dictionary: float32 [24576, 512], P(('fold', 'vox')), parts along dimension 0
- code_matrix: float32 [512, 512], P('fold'), parts along dimension 0
- dict_gram: float32 [1024, 512], P('fold'), parts along dimension 0
The draws below stay inside these ranges and needn't reach their ends.
There are 2 independent parts, one for each index of `fold`. The reference program is written for one: setup_inputs(seed, part) draws one part's arguments, and reference() takes and returns one part's arrays. A program takes and returns all parts, laid end to end along the dimension named above; an argument that names none is the same for every part. Nothing has to cross between parts.
All inputs are finite; a program needn't handle non-finite values.
Results may differ from the reference program's by a relative error of at most 0.0001.
Values sent between devices are 32-bit elements; how exact they have to be, the bound alone decides.
A program may use at most 64 MiB of HBM per device.

```python
import math
import jax
import jax.numpy as jnp
from jax import lax

ATOMS = 512
BATCH = 256
RECORDS = 512
FOLDS = 5
ISTA_STEPS = 5
DICT_STEPS = 2
VOXELS = 12288


def draw_dictionary(key, part):
    entry_key = jax.random.fold_in(key, 11)
    pick_key = jax.random.fold_in(key, 12)
    factor_key = jax.random.fold_in(key, 13)
    base = jnp.clip(jax.random.normal(entry_key, (VOXELS, ATOMS), jnp.float32), -6.0, 6.0)
    placing = jax.random.permutation(pick_key, ATOMS)
    weak_atom = placing < ATOMS // 8
    shrunk = jax.random.uniform(factor_key, (ATOMS,), jnp.float32, 0.15, 0.25)
    column_factor = jnp.where(weak_atom, shrunk, jnp.float32(1.0))
    return (base * column_factor[None, :] / math.sqrt(VOXELS)).astype(jnp.float32)


def touch_ends(result, rng, least, largest):
    spot = [jax.random.randint(jax.random.fold_in(rng, axis), (), 0, length) for axis, length in enumerate(result.shape)]
    widest = result.shape.index(max(result.shape))
    next_to = spot[:widest] + [(spot[widest] + 1) % result.shape[widest]] + spot[widest + 1:]
    return result.at[tuple(spot)].set(least).at[tuple(next_to)].set(largest)


def levels(rng, shape, split, low, high):
    factor_of = 1.0
    for dim, blocks in split:
        steps = jax.random.uniform(jax.random.fold_in(jax.random.fold_in(rng, 6), dim), (blocks,), jnp.float32, low / len(split), high / len(split))
        factor_of = factor_of * jnp.repeat(jnp.exp(steps), shape[dim] // blocks).reshape((-1,) + (1,) * (len(shape) - 1 - dim))
    return factor_of


def gaussian(rng, shape, spread, most, cuts=(), dtype=jnp.bfloat16):
    drawn = jax.random.normal(rng, shape, jnp.float32) * spread
    if len(cuts) > 0:
        drawn = levels(rng, shape, cuts, -0.22, 0.18) * drawn
    return jnp.clip(drawn, min=-most, max=most).astype(dtype)


def setup_inputs(seed: int = 0, part: int = 0) -> dict:
    key_of = jax.random.split(jax.random.key(seed), 6)
    part_keys = jax.random.split(jax.random.fold_in(key_of[5], part), 6)
    return {
        "volumes": gaussian(part_keys[0], (RECORDS, VOXELS), 1.0, 6.0, ((1, 16),), jnp.float32),
        "record_index": touch_ends(jax.random.randint(part_keys[1], (BATCH,), 0, RECORDS), jax.random.fold_in(part_keys[1], 1), 0, RECORDS - 1).astype(jnp.int32),
        "fold_of": touch_ends(jax.random.randint(part_keys[2], (RECORDS,), 0, FOLDS), jax.random.fold_in(part_keys[2], 1), 0, FOLDS - 1).astype(jnp.int32),
        "held_out": jax.random.randint(part_keys[3], (1,), 0, FOLDS).astype(jnp.int32),
        "dictionary": draw_dictionary(jax.random.fold_in(key_of[5], 71), part),
    }


penalty = 0.5

def matmul(left, right):
    return jnp.dot(left, right, precision=lax.Precision.HIGHEST, preferred_element_type=jnp.float32)

def row_bound(matrix):
    return jnp.max(lax.optimization_barrier(jnp.sum(jnp.abs(matrix), axis=1)))

def reference(volumes, record_index, fold_of, held_out, dictionary):
    batch_rows = volumes[record_index]
    weight = (fold_of[record_index] != held_out[0]).astype(jnp.float32)
    correlation = matmul(batch_rows, dictionary)
    gram_total = matmul(dictionary.T, dictionary)
    bound = row_bound(gram_total)
    code_rows = jnp.zeros_like(correlation)
    for sweep in range(ISTA_STEPS):
        moved = code_rows - (matmul(code_rows, gram_total) - correlation) / bound
        limit = penalty / bound
        code_rows = moved - jnp.clip(moved, -limit, limit)
    weighted = code_rows * weight[:, None]
    moment = matmul(code_rows.T, weighted)
    target = matmul(batch_rows.T, weighted)
    step_size = 1.0 / (1.0 + row_bound(moment))
    current = dictionary
    for sweep in range(DICT_STEPS):
        stepped = current - step_size * (matmul(current, moment) - target)
        lengths = jnp.sqrt(lax.optimization_barrier(jnp.sum(stepped * stepped, axis=0)))
        current = stepped / jnp.maximum(lengths, 1.0)
    dict_gram = matmul(current.T, current)
    return (current, code_rows, dict_gram)
```

```python
import functools

import jax
import jax.numpy as jnp
from jax import lax
from jax.experimental import pallas as pl
from jax.experimental.pallas import tpu as pltpu
from jax.sharding import PartitionSpec as P

ISTA_STEPS = 5
PIECES = 3
LANES = 128

penalty = 0.5
MESH = pl.DeviceIdType.MESH


def dot(left, right, dims):
    return lax.dot_general(
        left, right, (dims, ((), ())), precision=lax.Precision.HIGH, preferred_element_type=jnp.float32
    )


def row_bound(matrix):
    return jnp.max(jnp.sum(jnp.abs(matrix), axis=1))


def reduce_kernel(n, x_ref, out_ref, got0, sum0, got1, sum1, got2, sem0, sem1, sem2, gat2, gat1, gat0):
    me = lax.axis_index("vox")
    low, mid, high = lax.rem(me, 2), lax.rem(me // 2, 2), me // 4
    peers = n // 4
    half, quarter = n // 2, n // 4
    mate0 = me + 1 - 2 * low
    mate1 = me + 2 - 4 * mid
    there = [lax.rem(high + step, peers) for step in range(1, peers)]
    back = [lax.rem(high + peers - step, peers) for step in range(1, peers)]
    place = low * half + mid * quarter
    own = place + high

    def device(z):
        return {"vox": z * 4 + mid * 2 + low}

    def copy(src, dst, sems, index, to):
        return pltpu.make_async_remote_copy(
            src_ref=src, dst_ref=dst, send_sem=sems.at[(0,) + index], recv_sem=sems.at[(1,) + index],
            device_id=to, device_id_type=MESH,
        )

    barrier = pltpu.get_barrier_semaphore()
    for to in [{"vox": mate0}, {"vox": mate1}] + [device(z) for z in there]:
        pl.semaphore_signal(barrier, inc=1, device_id=to, device_id_type=MESH)
    pl.semaphore_wait(barrier, 2 + len(there))

    sends = []
    first = []
    for k in range(PIECES):
        c = copy(x_ref.at[k, pl.ds((1 - low) * half, half)], got0.at[k], sem0, (k,), {"vox": mate0})
        c.start()
        first.append(c)
    second = []
    for k in range(PIECES):
        first[k].wait_recv()
        sum0[k] = x_ref[k, pl.ds(low * half, half)] + got0[k]
        c = copy(sum0.at[k, pl.ds((1 - mid) * quarter, quarter)], got1.at[k], sem1, (k,), {"vox": mate1})
        c.start()
        second.append(c)
    third = []
    for k in range(PIECES):
        second[k].wait_recv()
        sum1[k] = sum0[k, pl.ds(mid * quarter, quarter)] + got1[k]
        for step, z in enumerate(there):
            c = copy(sum1.at[k, z], got2.at[k, step], sem2, (k, step), device(z))
            c.start()
            third.append(c)
    for k in range(PIECES):
        total = sum1[k, high]
        for step in range(peers - 1):
            third[k * (peers - 1) + step].wait_recv()
            total = total + got2[k, step]
        out_ref[k, own] = total
        for step, z in enumerate(there):
            c = copy(out_ref.at[k, own], out_ref.at[k, own], gat2, (k, step), device(z))
            c.start()
            sends.append(c)
    for k in range(PIECES):
        for step, z in enumerate(back):
            spot = out_ref.at[k, place + z]
            copy(spot, spot, gat2, (k, step), device(z)).wait_recv()
        spot = out_ref.at[k, pl.ds(place, quarter)]
        c = copy(spot, spot, gat1, (k,), {"vox": mate1})
        c.start()
        sends.append(c)
    for k in range(PIECES):
        spot = out_ref.at[k, pl.ds(low * half + (1 - mid) * quarter, quarter)]
        copy(spot, spot, gat1, (k,), {"vox": mate1}).wait_recv()
        spot = out_ref.at[k, pl.ds(low * half, half)]
        c = copy(spot, spot, gat0, (k,), {"vox": mate0})
        c.start()
        sends.append(c)
    for k in range(PIECES):
        spot = out_ref.at[k, pl.ds((1 - low) * half, half)]
        copy(spot, spot, gat0, (k,), {"vox": mate0}).wait_recv()
    for c in first + second + third + sends:
        c.wait_send()


def all_sum(n, flat):
    rows = flat.shape[0]
    chunk = -(-rows // (PIECES * n * 8)) * 8
    padded = PIECES * n * chunk
    if padded != rows:
        flat = jnp.pad(flat, ((0, padded - rows), (0, 0)))
    peers = n // 4
    shape = (PIECES, n, chunk, LANES)
    sem = pltpu.SemaphoreType.DMA
    out = pl.pallas_call(
        functools.partial(reduce_kernel, n),
        out_shape=jax.ShapeDtypeStruct(shape, jnp.float32),
        in_specs=[pl.BlockSpec(memory_space=pltpu.VMEM)],
        out_specs=pl.BlockSpec(memory_space=pltpu.VMEM),
        scratch_shapes=[
            pltpu.VMEM((PIECES, n // 2, chunk, LANES), jnp.float32),
            pltpu.VMEM((PIECES, n // 2, chunk, LANES), jnp.float32),
            pltpu.VMEM((PIECES, n // 4, chunk, LANES), jnp.float32),
            pltpu.VMEM((PIECES, n // 4, chunk, LANES), jnp.float32),
            pltpu.VMEM((PIECES, peers, chunk, LANES), jnp.float32),
            sem((2, PIECES)), sem((2, PIECES)), sem((2, PIECES, peers)),
            sem((2, PIECES, peers)), sem((2, PIECES)), sem((2, PIECES)),
        ],
        compiler_params=pltpu.CompilerParams(collective_id=0, has_side_effects=True),
    )(flat.reshape(shape))
    return out.reshape(padded, LANES)[:rows]


def pairs(tiles):
    return [(i, j) for i in range(tiles) for j in range(i, tiles)]


def pack(matrix):
    tiles = matrix.shape[0] // LANES
    return jnp.concatenate(
        [matrix[i * LANES:(i + 1) * LANES, j * LANES:(j + 1) * LANES] for i, j in pairs(tiles)], axis=0
    )


def unpack(flat, tiles):
    where = {pair: k for k, pair in enumerate(pairs(tiles))}

    def tile(i, j):
        if i > j:
            return tile(j, i).T
        k = where[(i, j)]
        return flat[k * LANES:(k + 1) * LANES]

    return jnp.concatenate(
        [jnp.concatenate([tile(i, j) for j in range(tiles)], axis=1) for i in range(tiles)], axis=0
    )


def shards(n, volumes, record_index, fold_of, held_out, dictionary):
    atoms = dictionary.shape[1]
    batch_rows = volumes[record_index]
    weight = (fold_of[record_index] != held_out[0]).astype(jnp.float32)
    joint = jnp.concatenate([dictionary, batch_rows.T], axis=1)
    part = dot(joint, joint, ((0,), (0,)))
    whole = unpack(all_sum(n, pack(part)), part.shape[0] // LANES)
    gram, correlation = whole[:atoms, :atoms], whole[atoms:, :atoms]
    bound = row_bound(gram)
    limit = penalty / bound
    moved = correlation / bound
    codes = moved - jnp.clip(moved, -limit, limit)
    for sweep in range(ISTA_STEPS - 1):
        moved = codes - (dot(codes, gram, ((1,), (0,))) - correlation) / bound
        codes = moved - jnp.clip(moved, -limit, limit)
    weighted = codes * weight[:, None]
    moment = dot(codes, weighted, ((0,), (0,)))
    step_size = 1.0 / (1.0 + row_bound(moment))
    scaled = step_size * weighted
    shift = step_size * moment
    side = dot(whole[:, atoms:], scaled, ((1,), (0,)))
    image = whole[:, :atoms]
    image = image - dot(image, shift, ((1,), (0,))) + side
    top = jnp.eye(atoms, dtype=jnp.float32) - shift
    length = jnp.sum(top * image[:atoms], axis=0) + jnp.sum(scaled * image[atoms:], axis=0)
    divisor = jnp.maximum(jnp.sqrt(jnp.maximum(length, 0.0)), 1.0)
    both = jnp.concatenate([top, scaled, image], axis=0) / divisor
    both = both - dot(both, shift, ((1,), (0,)))
    size = whole.shape[0]
    mix = jnp.concatenate([both[:atoms], both[atoms:size] + scaled], axis=0)
    image = both[size:] + side
    raw_gram = dot(mix, image, ((0,), (0,)))
    divisor = jnp.maximum(jnp.sqrt(jnp.maximum(jnp.diagonal(raw_gram), 0.0)), 1.0)
    current = dot(joint, mix, ((1,), (0,))) / divisor
    dict_gram = raw_gram / (divisor[:, None] * divisor[None, :])
    return (current, codes, dict_gram)


def solution(mesh):
    in_specs = (P("fold", "vox"), P("fold"), P("fold"), P("fold"), P("vox", None))
    out_specs = (P(("fold", "vox"), None), P("fold", None), P("fold", None))
    return jax.shard_map(
        functools.partial(shards, mesh.shape["vox"]), mesh=mesh, in_specs=in_specs, out_specs=out_specs, check_vma=False
    )
```

```python
import functools

import jax
import jax.numpy as jnp
from jax import lax
from jax.experimental import pallas as pl
from jax.experimental.pallas import tpu as pltpu
from jax.sharding import PartitionSpec as P

ISTA_STEPS = 5
PIECES = 3
LANES = 128
STRIP = 256

penalty = 0.5
MESH = pl.DeviceIdType.MESH
ROWS = ((1,), (0,))
CROSS = ((0,), (0,))


def split(value):
    high = value.astype(jnp.bfloat16)
    return high, (value - high.astype(jnp.float32)).astype(jnp.bfloat16)


def dot(left, right, dims=ROWS):
    return lax.dot_general(left, right, (dims, ((), ())), preferred_element_type=jnp.float32)


def dot3(left, right, dims=ROWS):
    return dot(left[0], right[0], dims) + (dot(left[0], right[1], dims) + dot(left[1], right[0], dims))


def pairs(tiles):
    return [(i, j) for i in range(tiles) for j in range(i, tiles)]


def column_of(row):
    return jnp.broadcast_to(row, (LANES, row.shape[1])).T[:, :1]


def match(index_ref, records):
    column = column_of(index_ref[...])
    return lax.broadcasted_iota(jnp.int32, (column.shape[0], records), 1) == column


def reduce_kernel(
    n, chunk, index_ref, vol_ref, dict_ref, out_ref, high_out, low_out,
    joint_h, joint_l, turned_h, turned_l, x_ref, got0, sum0, got1, sum1, got2,
    sem0, sem1, sem2, gat2, gat1, gat0, keep,
):
    me = lax.axis_index("vox")
    low, mid, high = lax.rem(me, 2), lax.rem(me // 2, 2), me // 4
    peers = n // 4
    half, quarter = n // 2 * chunk, n // 4 * chunk
    mate0 = {"vox": me + 1 - 2 * low}
    mate1 = {"vox": me + 2 - 4 * mid}
    there = [lax.rem(high + step, peers) for step in range(1, peers)]
    back = [lax.rem(high + peers - step, peers) for step in range(1, peers)]

    def at(start, size):
        return pl.ds(pl.multiple_of(start, 8), size)

    place = low * half + mid * quarter
    own = at(place + high * chunk, chunk)

    def device(z):
        return {"vox": z * 4 + mid * 2 + low}

    def copy(src, dst, sems, index, to):
        return pltpu.make_async_remote_copy(
            src_ref=src, dst_ref=dst, send_sem=sems.at[(0,) + index], recv_sem=sems.at[(1,) + index],
            device_id=to, device_id_type=MESH,
        )

    barrier = pltpu.get_barrier_semaphore()
    for to in [mate0, mate1] + [device(z) for z in there]:
        pl.semaphore_signal(barrier, inc=1, device_id=to, device_id_type=MESH)

    atoms = dict_ref.shape[1]
    size = joint_h.shape[1]
    picked = jnp.where(match(index_ref, vol_ref.shape[0]), 1.0, 0.0).astype(jnp.bfloat16)
    for part, joint, turned in zip(split(vol_ref[...]), (joint_h, joint_l), (turned_h, turned_l)):
        rows = dot(picked, part).astype(jnp.bfloat16)
        turned[atoms:] = rows
        joint[:, atoms:] = rows.T
    for part, joint, turned in zip(split(dict_ref[...]), (joint_h, joint_l), (turned_h, turned_l)):
        joint[:, :atoms] = part
        turned[:atoms] = part.T
    saves = [
        pltpu.make_async_copy(joint_h, high_out, keep.at[0]),
        pltpu.make_async_copy(joint_l, low_out, keep.at[1]),
    ]
    for c in saves:
        c.start()

    tiles = size // LANES
    per_piece = n * chunk // LANES
    order = {pair: t for t, pair in enumerate(pairs(tiles))}
    for t in range(len(order), PIECES * per_piece):
        x_ref[t // per_piece, pl.ds(t % per_piece * LANES, LANES)] = jnp.zeros((LANES, LANES), jnp.float32)
    first = []

    def send_first(k):
        if k == 0:
            pl.semaphore_wait(barrier, 2 + len(there))
        c = copy(x_ref.at[k, at((1 - low) * half, half)], got0.at[k], sem0, (k,), mate0)
        c.start()
        first.append(c)

    done = 0
    for top in range(0, size, STRIP):
        strip = dot3(
            (turned_h[top:top + STRIP], turned_l[top:top + STRIP]), (joint_h[:, top:], joint_l[:, top:])
        )
        for i in range(top // LANES, (top + STRIP) // LANES):
            for j in range(i, tiles):
                t = order[(i, j)]
                x_ref[t // per_piece, pl.ds(t % per_piece * LANES, LANES)] = strip[
                    i * LANES - top:(i + 1) * LANES - top, j * LANES - top:(j + 1) * LANES - top
                ]
                done += 1
        while len(first) < PIECES and (done >= (len(first) + 1) * per_piece or done == len(order)):
            send_first(len(first))

    sends = []
    second = []
    for k in range(PIECES):
        first[k].wait_recv()
        sum0[k] = x_ref[k, at(low * half, half)] + got0[k]
        c = copy(sum0.at[k, at((1 - mid) * quarter, quarter)], got1.at[k], sem1, (k,), mate1)
        c.start()
        second.append(c)
    third = []
    for k in range(PIECES):
        second[k].wait_recv()
        sum1[k] = sum0[k, at(mid * quarter, quarter)] + got1[k]
        for step, z in enumerate(there):
            c = copy(sum1.at[k, at(z * chunk, chunk)], got2.at[k, step], sem2, (k, step), device(z))
            c.start()
            third.append(c)
    for k in range(PIECES):
        total = sum1[k, at(high * chunk, chunk)]
        for step in range(peers - 1):
            third[k * (peers - 1) + step].wait_recv()
            total = total + got2[k, step]
        out_ref[k, own] = total
        for step, z in enumerate(there):
            c = copy(out_ref.at[k, own], out_ref.at[k, own], gat2, (k, step), device(z))
            c.start()
            sends.append(c)
    for k in range(PIECES):
        for step, z in enumerate(back):
            spot = out_ref.at[k, at(place + z * chunk, chunk)]
            copy(spot, spot, gat2, (k, step), device(z)).wait_recv()
        spot = out_ref.at[k, at(place, quarter)]
        c = copy(spot, spot, gat1, (k,), mate1)
        c.start()
        sends.append(c)
    for k in range(PIECES):
        spot = out_ref.at[k, at(low * half + (1 - mid) * quarter, quarter)]
        copy(spot, spot, gat1, (k,), mate1).wait_recv()
        spot = out_ref.at[k, at(low * half, half)]
        c = copy(spot, spot, gat0, (k,), mate0)
        c.start()
        sends.append(c)
    for k in range(PIECES):
        spot = out_ref.at[k, at((1 - low) * half, half)]
        copy(spot, spot, gat0, (k,), mate0).wait_recv()
    for c in first + second + third + sends:
        c.wait_send()
    for c in saves:
        c.wait()


def joint_gram(n, record_index, volumes, dictionary):
    voxels, atoms = dictionary.shape
    size = atoms + record_index.shape[1]
    rows = len(pairs(size // LANES)) * LANES
    chunk = -(-rows // (PIECES * n * 8)) * 8
    peers = n // 4
    sem = pltpu.SemaphoreType.DMA
    vmem = pl.BlockSpec(memory_space=pltpu.VMEM)
    anywhere = pl.BlockSpec(memory_space=pl.ANY)
    return pl.pallas_call(
        functools.partial(reduce_kernel, n, chunk),
        out_shape=(
            jax.ShapeDtypeStruct((PIECES, n * chunk, LANES), jnp.float32),
            jax.ShapeDtypeStruct((voxels, size), jnp.bfloat16),
            jax.ShapeDtypeStruct((voxels, size), jnp.bfloat16),
        ),
        in_specs=[vmem] * 3,
        out_specs=(vmem, anywhere, anywhere),
        scratch_shapes=[
            pltpu.VMEM((voxels, size), jnp.bfloat16),
            pltpu.VMEM((voxels, size), jnp.bfloat16),
            pltpu.VMEM((size, voxels), jnp.bfloat16),
            pltpu.VMEM((size, voxels), jnp.bfloat16),
            pltpu.VMEM((PIECES, n * chunk, LANES), jnp.float32),
            pltpu.VMEM((PIECES, n // 2 * chunk, LANES), jnp.float32),
            pltpu.VMEM((PIECES, n // 2 * chunk, LANES), jnp.float32),
            pltpu.VMEM((PIECES, n // 4 * chunk, LANES), jnp.float32),
            pltpu.VMEM((PIECES, n // 4 * chunk, LANES), jnp.float32),
            pltpu.VMEM((PIECES, peers, chunk, LANES), jnp.float32),
            sem((2, PIECES)), sem((2, PIECES)), sem((2, PIECES, peers)),
            sem((2, PIECES, peers)), sem((2, PIECES)), sem((2, PIECES)),
            sem((2,)),
        ],
        compiler_params=pltpu.CompilerParams(collective_id=0, has_side_effects=True),
    )(record_index, volumes, dictionary)


def update_kernel(
    flat_ref, index_ref, fold_ref, held_ref, high_in, low_in, new_out, code_out, gram_out,
    full, full_h, full_l, joint_h, joint_l, both, side_ref, new_ref, code_ref, gram_ref, sems,
):
    size = full.shape[0]
    batch, atoms = code_ref.shape
    voxels = joint_h.shape[0]
    loads = [
        pltpu.make_async_copy(high_in, joint_h, sems.at[0]),
        pltpu.make_async_copy(low_in, joint_l, sems.at[1]),
    ]
    for c in loads:
        c.start()
    per_piece = flat_ref.shape[1] // LANES
    for t, (i, j) in enumerate(pairs(size // LANES)):
        tile = flat_ref[t // per_piece, pl.ds(t % per_piece * LANES, LANES)]
        spots = [(i, j, tile)] + ([(j, i, tile.T)] if j > i else [])
        for row, column, value in spots:
            where = (pl.ds(row * LANES, LANES), pl.ds(column * LANES, LANES))
            full[where] = value
            full_h[where], full_l[where] = split(value)
    bound = jnp.max(jnp.sum(jnp.abs(full[:atoms, :atoms]), axis=0))
    limit = penalty / bound
    gram = (full_h[:atoms, :atoms], full_l[:atoms, :atoms])
    correlation = full[atoms:, :atoms]
    moved = correlation / bound
    codes = moved - jnp.clip(moved, -limit, limit)
    for sweep in range(ISTA_STEPS - 1):
        moved = codes - (dot3(split(codes), gram) - correlation) / bound
        codes = moved - jnp.clip(moved, -limit, limit)
    code_ref[...] = codes
    stores = [pltpu.make_async_copy(code_ref, code_out, sems.at[2])]
    stores[0].start()
    folds = jnp.sum(jnp.where(match(index_ref, fold_ref.shape[1]), fold_ref[...], 0), axis=1, keepdims=True)
    weight = jnp.where(folds != held_ref[0], 1.0, 0.0)
    weighted = codes * weight
    moment = dot3(split(codes), split(weighted), CROSS)
    step_size = 1.0 / (1.0 + jnp.max(jnp.sum(jnp.abs(moment), axis=0)))
    scaled = step_size * weighted
    shift = step_size * moment
    shift_parts = split(shift)
    scaled_parts = split(scaled)
    side = dot3((full_h[:, atoms:], full_l[:, atoms:]), scaled_parts)
    side_ref[...] = side
    image = full[:, :atoms] - dot3((full_h[:, :atoms], full_l[:, :atoms]), shift_parts) + side
    both[size:] = image
    diagonal = lax.broadcasted_iota(jnp.int32, (atoms, atoms), 0) == lax.broadcasted_iota(
        jnp.int32, (atoms, atoms), 1
    )
    both[:atoms] = jnp.where(diagonal, 1.0, 0.0) - shift
    both[atoms:size] = scaled
    length = jnp.sum(both[:size] * both[size:], axis=0, keepdims=True)
    inverse = 1.0 / jnp.maximum(jnp.sqrt(jnp.maximum(length, 0.0)), 1.0)
    for top in range(0, 2 * size, STRIP):
        rows = pl.ds(top, STRIP)
        value = both[rows] * inverse
        value = value - dot3(split(value), shift_parts)
        if top >= size:
            value = value + side_ref[pl.ds(top - size, STRIP)]
        elif top >= atoms:
            value = value + scaled[top - atoms:top - atoms + STRIP]
        both[rows] = value
    length = jnp.sum(both[:size] * both[size:], axis=0, keepdims=True)
    inverse = 1.0 / jnp.maximum(jnp.sqrt(jnp.maximum(length, 0.0)), 1.0)
    mix = split(both[:size] * inverse)
    for c in loads:
        c.wait()
    for k, top in enumerate(range(0, voxels, STRIP)):
        rows = pl.ds(top, STRIP)
        new_ref[rows] = dot3((joint_h[rows], joint_l[rows]), mix)
        c = pltpu.make_async_copy(new_ref.at[rows], new_out.at[rows], sems.at[4 + k])
        c.start()
        stores.append(c)
    gram_ref[...] = dot3(mix, split(both[size:] * inverse), CROSS)
    c = pltpu.make_async_copy(gram_ref, gram_out, sems.at[3])
    c.start()
    stores.append(c)
    for c in stores:
        c.wait()


def update(flat, record_index, fold_of, held_out, joint_h, joint_l, atoms):
    voxels, size = joint_h.shape
    batch = record_index.shape[1]
    vmem = pl.BlockSpec(memory_space=pltpu.VMEM)
    anywhere = pl.BlockSpec(memory_space=pl.ANY)
    return pl.pallas_call(
        update_kernel,
        out_shape=(
            jax.ShapeDtypeStruct((voxels, atoms), jnp.float32),
            jax.ShapeDtypeStruct((batch, atoms), jnp.float32),
            jax.ShapeDtypeStruct((atoms, atoms), jnp.float32),
        ),
        in_specs=[vmem, vmem, vmem, pl.BlockSpec(memory_space=pltpu.SMEM), anywhere, anywhere],
        out_specs=(anywhere, anywhere, anywhere),
        scratch_shapes=[
            pltpu.VMEM((size, size), jnp.float32),
            pltpu.VMEM((size, size), jnp.bfloat16),
            pltpu.VMEM((size, size), jnp.bfloat16),
            pltpu.VMEM((voxels, size), jnp.bfloat16),
            pltpu.VMEM((voxels, size), jnp.bfloat16),
            pltpu.VMEM((2 * size, atoms), jnp.float32),
            pltpu.VMEM((size, atoms), jnp.float32),
            pltpu.VMEM((voxels, atoms), jnp.float32),
            pltpu.VMEM((batch, atoms), jnp.float32),
            pltpu.VMEM((atoms, atoms), jnp.float32),
            pltpu.SemaphoreType.DMA((4 + voxels // STRIP,)),
        ],
    )(flat, record_index, fold_of, held_out, joint_h, joint_l)


def shards(n, volumes, record_index, fold_of, held_out, dictionary):
    record_index = record_index.reshape(1, -1)
    flat, joint_h, joint_l = joint_gram(n, record_index, volumes, dictionary)
    return update(flat, record_index, fold_of.reshape(1, -1), held_out, joint_h, joint_l, dictionary.shape[1])


def solution(mesh):
    in_specs = (P("fold", "vox"), P("fold"), P("fold"), P("fold"), P("vox", None))
    out_specs = (P(("fold", "vox"), None), P("fold", None), P("fold", None))
    return jax.shard_map(
        functools.partial(shards, mesh.shape["vox"]), mesh=mesh, in_specs=in_specs, out_specs=out_specs, check_vma=False
    )
```

```python
import functools

import jax
import jax.numpy as jnp
from jax import lax
from jax.experimental import pallas as pl
from jax.experimental.pallas import tpu as pltpu
from jax.sharding import PartitionSpec as P

ISTA_STEPS = 5
PIECES = 3
SLOPE = 8
LANES = 128
STRIP = 256

penalty = 0.5
MESH = pl.DeviceIdType.MESH
ROWS = ((1,), (0,))
CROSS = ((0,), (0,))


def split(value):
    high = value.astype(jnp.bfloat16)
    return high, (value - high.astype(jnp.float32)).astype(jnp.bfloat16)


def dot(left, right, dims=ROWS):
    return lax.dot_general(left, right, (dims, ((), ())), preferred_element_type=jnp.float32)


def dot3(left, right, dims=ROWS):
    return dot(left[0], right[0], dims) + (dot(left[0], right[1], dims) + dot(left[1], right[0], dims))


def pairs(tiles):
    return [(i, j) for i in range(tiles) for j in range(i, tiles)]


def column_of(row):
    return jnp.broadcast_to(row, (LANES, row.shape[1])).T[:, :1]


def match(index_ref, records):
    column = column_of(index_ref[...])
    return lax.broadcasted_iota(jnp.int32, (column.shape[0], records), 1) == column


def sequence(atom_tiles, tiles):
    within = [(i, j) for i, j in pairs(atom_tiles)]
    across = [(i, j) for i in range(atom_tiles) for j in range(atom_tiles, tiles)]
    return within + across + [(i, j) for i, j in pairs(tiles) if i >= atom_tiles]


def bit_order(piece, bits):
    order = list(range(bits))
    if piece % 4 == 1:
        order[1], order[2] = 2, 1
    return order


def reduce_kernel(
    n, chunk, index_ref, vol_in, dict_in, out_ref, high_out, low_out,
    vol_ref, dict_ref, joint_h, joint_l, turned_h, turned_l, x_ref, got, sems, keep,
):
    me = lax.axis_index("vox")
    bits = n.bit_length() - 1
    bit = [lax.rem(me // 2 ** b, 2) for b in range(bits)]
    mate = [{"vox": me + (1 - 2 * bit[b]) * 2 ** b} for b in range(bits)]
    rows = n * chunk
    loads = [
        pltpu.make_async_copy(dict_in, dict_ref, keep.at[2]),
        pltpu.make_async_copy(vol_in, vol_ref, keep.at[3]),
    ]
    for c in loads:
        c.start()
    barrier = pltpu.get_barrier_semaphore()
    for to in mate:
        pl.semaphore_signal(barrier, inc=1, device_id=to, device_id_type=MESH)

    def at(start, size):
        return pl.ds(pl.multiple_of(start, 8), size)

    starts = []
    for k in range(PIECES):
        start, path = 0, [0]
        for s, b in enumerate(bit_order(k, bits)):
            start = start + bit[b] * (rows >> (s + 1))
            path.append(start)
        starts.append(path)

    copies = {}

    def send(k, t):
        gathers = t >= bits
        s = 2 * bits - 1 - t if gathers else t
        b = bit_order(k, bits)[s]
        half = rows >> (s + 1)
        if gathers:
            src = dst = out_ref.at[k, at(starts[k][s + 1], half)]
        else:
            src = x_ref.at[k, at(starts[k][s] + (1 - bit[b]) * half, half)]
            dst = got.at[k, pl.ds(rows - (rows >> s), half)]
        c = pltpu.make_async_remote_copy(
            src_ref=src, dst_ref=dst, send_sem=sems.at[0, t, k], recv_sem=sems.at[1, t, k],
            device_id=mate[b], device_id_type=MESH,
        )
        c.start()
        copies[(k, t)] = c

    def advance(k, t):
        if t <= bits:
            copies[(k, t - 1)].wait_recv()
            half = rows >> t
            spot = at(starts[k][t], half)
            value = x_ref[k, spot] + got[k, pl.ds(rows - (rows >> (t - 1)), half)]
            if t == bits:
                out_ref[k, spot] = value
            else:
                x_ref[k, spot] = value
        else:
            s = 2 * bits - t
            b = bit_order(k, bits)[s]
            half = rows >> (s + 1)
            spot = out_ref.at[k, at(starts[k][s] + (1 - bit[b]) * half, half)]
            pltpu.make_async_remote_copy(
                src_ref=spot, dst_ref=spot, send_sem=sems.at[0, t - 1, k], recv_sem=sems.at[1, t - 1, k],
                device_id=mate[b], device_id_type=MESH,
            ).wait_recv()
        if t < 2 * bits:
            send(k, t)

    atoms = dict_ref.shape[1]
    size = joint_h.shape[1]
    tiles = size // LANES
    per_piece = rows // LANES
    order = {pair: t for t, pair in enumerate(sequence(atoms // LANES, tiles))}
    for t in range(len(order), PIECES * per_piece):
        x_ref[t // per_piece, pl.ds(t % per_piece * LANES, LANES)] = jnp.zeros((LANES, LANES), jnp.float32)
    stored = set()
    begun = []
    finished = set()

    def store(top, left, strip):
        for i in range(top // LANES, (top + strip.shape[0]) // LANES):
            for j in range(max(i, left // LANES), (left + strip.shape[1]) // LANES):
                t = order[(i, j)]
                x_ref[t // per_piece, pl.ds(t % per_piece * LANES, LANES)] = strip[
                    i * LANES - top:(i + 1) * LANES - top, j * LANES - left:(j + 1) * LANES - left
                ]
                stored.add(t)
        for k in range(len(begun), PIECES):
            if all(t in stored or t >= len(order) for t in range(k * per_piece, (k + 1) * per_piece)):
                if k == 0:
                    pl.semaphore_wait(barrier, bits)
                begun.append(k)
                send(k, 0)
            else:
                break

    def gram(top, height, left, right):
        store(top, left, dot3(
            (turned_h[top:top + height], turned_l[top:top + height]),
            (joint_h[:, left:right], joint_l[:, left:right]),
        ))

    def pump(steps):
        for t in range(1, steps + 1):
            for k in begun:
                if (k, t) not in finished:
                    finished.add((k, t))
                    advance(k, t)

    loads[0].wait()
    for part, joint, turned in zip(split(dict_ref[...]), (joint_h, joint_l), (turned_h, turned_l)):
        joint[:, :atoms] = part
        turned[:atoms] = part.T
    for top in range(0, atoms, STRIP):
        gram(top, STRIP, top, atoms)
    loads[1].wait()
    picked = jnp.where(match(index_ref, vol_ref.shape[0]), 1.0, 0.0).astype(jnp.bfloat16)
    for part, joint, turned in zip(split(vol_ref[...]), (joint_h, joint_l), (turned_h, turned_l)):
        picks = dot(picked, part).astype(jnp.bfloat16)
        turned[atoms:] = picks
        joint[:, atoms:] = picks.T
    pump(1)
    for top in range(0, atoms, STRIP):
        gram(top, STRIP, atoms, size)
        pump(1)
    gram(atoms, size - atoms, atoms, size)
    saves = [
        pltpu.make_async_copy(joint_h, high_out, keep.at[0]),
        pltpu.make_async_copy(joint_l, low_out, keep.at[1]),
    ]
    for c in saves:
        c.start()
    tasks = [(k, t) for k in range(PIECES) for t in range(1, 2 * bits + 1) if (k, t) not in finished]
    for k, t in sorted(tasks, key=lambda task: (task[0] + SLOPE * task[1], -task[1])):
        advance(k, t)
    for c in copies.values():
        c.wait_send()
    for c in saves:
        c.wait()


def joint_gram(n, record_index, volumes, dictionary):
    voxels, atoms = dictionary.shape
    size = atoms + record_index.shape[1]
    rows = len(pairs(size // LANES)) * LANES
    chunk = -(-rows // (PIECES * n * 8)) * 8
    bits = n.bit_length() - 1
    sem = pltpu.SemaphoreType.DMA
    vmem = pl.BlockSpec(memory_space=pltpu.VMEM)
    anywhere = pl.BlockSpec(memory_space=pl.ANY)
    return pl.pallas_call(
        functools.partial(reduce_kernel, n, chunk),
        out_shape=(
            jax.ShapeDtypeStruct((PIECES, n * chunk, LANES), jnp.float32),
            jax.ShapeDtypeStruct((voxels, size), jnp.bfloat16),
            jax.ShapeDtypeStruct((voxels, size), jnp.bfloat16),
        ),
        in_specs=[vmem, anywhere, anywhere],
        out_specs=(vmem, anywhere, anywhere),
        scratch_shapes=[
            pltpu.VMEM(volumes.shape, jnp.float32),
            pltpu.VMEM(dictionary.shape, jnp.float32),
            pltpu.VMEM((voxels, size), jnp.bfloat16),
            pltpu.VMEM((voxels, size), jnp.bfloat16),
            pltpu.VMEM((size, voxels), jnp.bfloat16),
            pltpu.VMEM((size, voxels), jnp.bfloat16),
            pltpu.VMEM((PIECES, n * chunk, LANES), jnp.float32),
            pltpu.VMEM((PIECES, n * chunk, LANES), jnp.float32),
            sem((2, 2 * bits, PIECES)),
            sem((4,)),
        ],
        compiler_params=pltpu.CompilerParams(collective_id=0, has_side_effects=True),
    )(record_index, volumes, dictionary)


def update_kernel(
    flat_ref, index_ref, fold_ref, held_ref, high_in, low_in, new_out, code_out, gram_out,
    full, full_h, full_l, joint_h, joint_l, both, side_ref, new_ref, code_ref, gram_ref, sems,
):
    size = full.shape[0]
    batch, atoms = code_ref.shape
    voxels = joint_h.shape[0]
    loads = [
        pltpu.make_async_copy(high_in, joint_h, sems.at[0]),
        pltpu.make_async_copy(low_in, joint_l, sems.at[1]),
    ]
    for c in loads:
        c.start()
    per_piece = flat_ref.shape[1] // LANES
    for t, (i, j) in enumerate(sequence(atoms // LANES, size // LANES)):
        tile = flat_ref[t // per_piece, pl.ds(t % per_piece * LANES, LANES)]
        spots = [(i, j, tile)] + ([(j, i, tile.T)] if j > i else [])
        for row, column, value in spots:
            where = (pl.ds(row * LANES, LANES), pl.ds(column * LANES, LANES))
            full[where] = value
            full_h[where], full_l[where] = split(value)
    bound = jnp.max(jnp.sum(jnp.abs(full[:atoms, :atoms]), axis=0))
    limit = penalty / bound
    gram = (full_h[:atoms, :atoms], full_l[:atoms, :atoms])
    correlation = full[atoms:, :atoms]
    moved = correlation / bound
    codes = moved - jnp.clip(moved, -limit, limit)
    for sweep in range(ISTA_STEPS - 1):
        moved = codes - (dot3(split(codes), gram) - correlation) / bound
        codes = moved - jnp.clip(moved, -limit, limit)
    code_ref[...] = codes
    stores = [pltpu.make_async_copy(code_ref, code_out, sems.at[2])]
    stores[0].start()
    folds = jnp.sum(jnp.where(match(index_ref, fold_ref.shape[1]), fold_ref[...], 0), axis=1, keepdims=True)
    weight = jnp.where(folds != held_ref[0], 1.0, 0.0)
    weighted = codes * weight
    moment = dot3(split(codes), split(weighted), CROSS)
    step_size = 1.0 / (1.0 + jnp.max(jnp.sum(jnp.abs(moment), axis=0)))
    scaled = step_size * weighted
    shift = step_size * moment
    shift_parts = split(shift)
    scaled_parts = split(scaled)
    side = dot3((full_h[:, atoms:], full_l[:, atoms:]), scaled_parts)
    side_ref[...] = side
    image = full[:, :atoms] - dot3((full_h[:, :atoms], full_l[:, :atoms]), shift_parts) + side
    both[size:] = image
    diagonal = lax.broadcasted_iota(jnp.int32, (atoms, atoms), 0) == lax.broadcasted_iota(
        jnp.int32, (atoms, atoms), 1
    )
    both[:atoms] = jnp.where(diagonal, 1.0, 0.0) - shift
    both[atoms:size] = scaled
    length = jnp.sum(both[:size] * both[size:], axis=0, keepdims=True)
    inverse = 1.0 / jnp.maximum(jnp.sqrt(jnp.maximum(length, 0.0)), 1.0)
    for top in range(0, 2 * size, STRIP):
        rows = pl.ds(top, STRIP)
        value = both[rows] * inverse
        value = value - dot3(split(value), shift_parts)
        if top >= size:
            value = value + side_ref[pl.ds(top - size, STRIP)]
        elif top >= atoms:
            value = value + scaled[top - atoms:top - atoms + STRIP]
        both[rows] = value
    length = jnp.sum(both[:size] * both[size:], axis=0, keepdims=True)
    inverse = 1.0 / jnp.maximum(jnp.sqrt(jnp.maximum(length, 0.0)), 1.0)
    mix = split(both[:size] * inverse)
    for c in loads:
        c.wait()
    for k, top in enumerate(range(0, voxels, STRIP)):
        rows = pl.ds(top, STRIP)
        new_ref[rows] = dot3((joint_h[rows], joint_l[rows]), mix)
        c = pltpu.make_async_copy(new_ref.at[rows], new_out.at[rows], sems.at[4 + k])
        c.start()
        stores.append(c)
    gram_ref[...] = dot3(mix, split(both[size:] * inverse), CROSS)
    c = pltpu.make_async_copy(gram_ref, gram_out, sems.at[3])
    c.start()
    stores.append(c)
    for c in stores:
        c.wait()


def update(flat, record_index, fold_of, held_out, joint_h, joint_l, atoms):
    voxels, size = joint_h.shape
    batch = record_index.shape[1]
    vmem = pl.BlockSpec(memory_space=pltpu.VMEM)
    anywhere = pl.BlockSpec(memory_space=pl.ANY)
    return pl.pallas_call(
        update_kernel,
        out_shape=(
            jax.ShapeDtypeStruct((voxels, atoms), jnp.float32),
            jax.ShapeDtypeStruct((batch, atoms), jnp.float32),
            jax.ShapeDtypeStruct((atoms, atoms), jnp.float32),
        ),
        in_specs=[vmem, vmem, vmem, pl.BlockSpec(memory_space=pltpu.SMEM), anywhere, anywhere],
        out_specs=(anywhere, anywhere, anywhere),
        scratch_shapes=[
            pltpu.VMEM((size, size), jnp.float32),
            pltpu.VMEM((size, size), jnp.bfloat16),
            pltpu.VMEM((size, size), jnp.bfloat16),
            pltpu.VMEM((voxels, size), jnp.bfloat16),
            pltpu.VMEM((voxels, size), jnp.bfloat16),
            pltpu.VMEM((2 * size, atoms), jnp.float32),
            pltpu.VMEM((size, atoms), jnp.float32),
            pltpu.VMEM((voxels, atoms), jnp.float32),
            pltpu.VMEM((batch, atoms), jnp.float32),
            pltpu.VMEM((atoms, atoms), jnp.float32),
            pltpu.SemaphoreType.DMA((4 + voxels // STRIP,)),
        ],
    )(flat, record_index, fold_of, held_out, joint_h, joint_l)


def shards(n, volumes, record_index, fold_of, held_out, dictionary):
    record_index = record_index.reshape(1, -1)
    flat, joint_h, joint_l = joint_gram(n, record_index, volumes, dictionary)
    return update(flat, record_index, fold_of.reshape(1, -1), held_out, joint_h, joint_l, dictionary.shape[1])


def solution(mesh):
    in_specs = (P("fold", "vox"), P("fold"), P("fold"), P("fold"), P("vox", None))
    out_specs = (P(("fold", "vox"), None), P("fold", None), P("fold", None))
    return jax.shard_map(
        functools.partial(shards, mesh.shape["vox"]), mesh=mesh, in_specs=in_specs, out_specs=out_specs, check_vma=False
    )
```
